32 devices in a mesh: groups: 2 (over x), ctx: 16 (over z, y, core).
Axes of the slice: x: 2, y: 2, z: 4, core: 2. Of those that a mesh axis runs over, the one named last changes fastest.
Arguments:
- signal_spectrum: bfloat16 [2, 8192, 4096], P(None, ('groups', 'ctx')), parts along dimension 1, may hold values from -6 to 6
- filter_spectrum: bfloat16 [2, 4096, 4096], P(None, 'ctx'), may hold values from -6 to 6
- output_gate: bfloat16 [4096, 4096], P(('groups', 'ctx')), parts along dimension 0, may hold values from -8 to 8
- projection: bfloat16 [4096, 384], replicated, may hold values from -0.5 to 0.5
Outputs:
- attended: bfloat16 [4096, 128], P(('groups', 'ctx')), parts along dimension 0
The draws below stay inside these ranges and needn't reach their ends.
There are 2 independent parts, one for each index of `groups`. The reference program is written for one: setup_inputs(seed, part) draws one part's arguments, and reference() takes and returns one part's arrays. A program takes and returns all parts, laid end to end along the dimension named above; an argument that names none is the same for every part. Nothing has to cross between parts.
All inputs are finite; a program needn't handle non-finite values.
Results may differ from the reference program's by a relative error of at most 0.019.
Values may be sent and summed in bfloat16 or wider, within the bound.
No kernel may reach another device: no remote copies, remote signals or barrier semaphores. Data moves between devices by JAX's collectives and lax.ppermute only.
A program may use at most 128 MiB of HBM per device.

```python
import math
import jax
import jax.numpy as jnp
from jax import lax

D = 4096
HEAD = 128
SEQ = 2048
FREQS = 4096


def draw_output_gate(key, part):
    values = jax.random.normal(key, (SEQ, D), jnp.float32)
    return jnp.clip(values, -4.0, 4.0).astype(jnp.bfloat16)


def draw_projection(key, part):
    base = jax.random.normal(key, (D, 3 * HEAD), jnp.float32) / jnp.sqrt(jnp.float32(D))
    base = jnp.clip(base, -0.5, 0.5)
    return base.astype(jnp.bfloat16)


def shard_levels(key, shape, split, least, high):
    def one(position, blocks):
        heights = jax.random.uniform(jax.random.fold_in(jax.random.fold_in(key, 6), position), (blocks,), jnp.float32, least / len(split), high / len(split))
        return jnp.repeat(jnp.exp(heights), shape[position] // blocks).reshape((-1,) + (1,) * (len(shape) - position - 1))

    loudness = one(*split[0])
    for cut in split[1:]:
        loudness = loudness * one(*cut)
    return loudness


def gaussian(rng, shape, deviation, bound, split=(), held_as=jnp.bfloat16):
    array = jax.random.normal(rng, shape, jnp.float32) * deviation
    if len(split) > 0:
        array = shard_levels(rng, shape, split, -0.22, 0.18) * array
    return jnp.clip(array, min=-bound, max=bound).astype(held_as)


def setup_inputs(seed: int = 0, part: int = 0) -> dict:
    splits = jax.random.split(jax.random.key(seed), 5)
    part_splits = jax.random.split(jax.random.fold_in(splits[4], part), 5)
    return {
        "signal_spectrum": gaussian(part_splits[0], (2, FREQS, D), 1.0, 6.0, ((1, 16),)),
        "filter_spectrum": gaussian(splits[1], (2, FREQS, D), 1.0, 6.0, ((1, 16),)),
        "output_gate": draw_output_gate(jax.random.fold_in(jax.random.fold_in(splits[4], part), 71), part),
        "projection": draw_projection(jax.random.fold_in(splits[4], 71), part),
    }


def reference(signal_spectrum, filter_spectrum, output_gate, projection):
    slab_width = math.gcd(D, 256)

    def one_slab(slab_index):
        first_col = (slab_index * slab_width).astype(jnp.int32)
        signal = lax.dynamic_slice_in_dim(signal_spectrum, first_col, slab_width, 2).astype(jnp.float32)
        kernel = lax.dynamic_slice_in_dim(filter_spectrum, first_col, slab_width, 2).astype(jnp.float32)
        real_part = signal[0] * kernel[0] - signal[1] * kernel[1]
        imag_part = signal[0] * kernel[1] + signal[1] * kernel[0]
        spectrum = lax.complex(real_part, imag_part)
        return jnp.real(jnp.fft.ifft(spectrum, axis=0, norm='ortho'))[:SEQ]
    slabs = lax.map(one_slab, jnp.arange(D // slab_width, dtype=jnp.int32))
    mixed = jnp.transpose(slabs, (1, 0, 2)).reshape(SEQ, D)
    gated = (mixed * output_gate.astype(jnp.float32)).astype(jnp.bfloat16)
    packed = jnp.dot(gated, projection, preferred_element_type=jnp.float32)
    query = packed[:, :HEAD].astype(jnp.bfloat16)
    keys = packed[:, HEAD:2 * HEAD].astype(jnp.bfloat16)
    values = packed[:, 2 * HEAD:].astype(jnp.bfloat16)
    block_rows = math.gcd(SEQ, 1024)
    positions = jnp.arange(SEQ, dtype=jnp.int32)
    score_scale = 1.0 / math.sqrt(HEAD)

    def one_block(block_index):
        first_row = (block_index * block_rows).astype(jnp.int32)
        rows_here = lax.dynamic_slice_in_dim(query, first_row, block_rows, 0)
        scores = jnp.dot(rows_here, keys.T, preferred_element_type=jnp.float32) * score_scale
        row_pos = first_row + jnp.arange(block_rows, dtype=jnp.int32)
        allowed = positions[None, :] <= row_pos[:, None]
        scores = jnp.where(allowed, scores, -1e+30)
        row_max = lax.optimization_barrier(jnp.max(scores, axis=1, keepdims=True))
        exponents = jnp.where(allowed, jnp.exp(scores - row_max), 0.0)
        totals = lax.optimization_barrier(jnp.sum(exponents, axis=1, keepdims=True))
        weights = exponents.astype(jnp.bfloat16)
        result = jnp.dot(weights, values, preferred_element_type=jnp.float32) / totals
        return result.astype(jnp.bfloat16)
    blocks = lax.map(one_block, jnp.arange(SEQ // block_rows, dtype=jnp.int32))
    return blocks.reshape(SEQ, HEAD)
```

```python
import math

import jax
import jax.numpy as jnp
from jax import lax
from jax.experimental import pallas as pl
from jax.experimental.pallas import tpu as pltpu
from jax.sharding import PartitionSpec as P

TWO_PI = 2.0 * math.pi
FLOOR = -1e30
BF16 = jnp.bfloat16
F32 = jnp.float32
PLANES = 4
CHUNKS = (2, 2, 2, 2)


def unit_circle(numerator, modulus):
    phases = TWO_PI / modulus * (numerator % modulus).astype(F32)
    return jnp.cos(phases), jnp.sin(phases)


def times(left, right):
    return left[0] * right[0] - left[1] * right[1], left[0] * right[1] + left[1] * right[0]


def product_kernel(ids, *refs):
    signals, filters, outs = refs[:4], refs[4:8], refs[8:]
    for signal, kernel, out in zip(signals, filters, outs):
        s_re, s_im = signal[0].astype(F32), signal[1].astype(F32)
        k_re, k_im = kernel[0].astype(F32), kernel[1].astype(F32)
        out[0] = (s_re * k_re - s_im * k_im).astype(BF16)
        out[1] = (s_re * k_im + s_im * k_re).astype(BF16)


def products(ids, signal, kernel, offset, width):
    freqs = signal.shape[1]
    block = freqs // 2
    first = offset // width

    def piece(m):
        return pl.BlockSpec((2, block, width), lambda g, ids: (0, g, first + ids[m]))

    out = jax.ShapeDtypeStruct((2, freqs, width), BF16)
    return pl.pallas_call(
        product_kernel,
        out_shape=(out,) * 4,
        grid_spec=pltpu.PrefetchScalarGridSpec(
            num_scalar_prefetch=1,
            grid=(freqs // block,),
            in_specs=[piece(m) for m in range(4)] * 2,
            out_specs=[pl.BlockSpec((2, block, width), lambda g, ids: (0, g, 0))] * 4,
        ),
        cost_estimate=pl.CostEstimate(
            flops=24 * freqs * width, bytes_accessed=48 * freqs * width, transcendentals=0
        ),
        name="products",
    )(ids, *([signal] * 4), *([kernel] * 4))


def transform_kernel(table, p0, p1, p2, p3, out_a, out_b, out_own):
    step = pl.program_id(0)
    depth = p0.shape[0] * p0.shape[1]
    total = None
    for m, piece in enumerate((p0, p1, p2, p3)):
        term = jnp.dot(
            table[:, m * depth : (m + 1) * depth],
            piece[...].reshape(depth, piece.shape[2]),
            preferred_element_type=F32,
        )
        total = term if total is None else total + term

    @pl.when(step < 4)
    def _():
        out_a[0] = total.astype(BF16)

    @pl.when((step >= 4) & (step < 6))
    def _():
        out_b[...] = total.astype(BF16)

    @pl.when(step >= 6)
    def _():
        out_own[...] = total


def transform(table, pieces):
    width = pieces[0].shape[2]
    span, depth = table.shape
    rows = span // 4
    half = rows // 2
    whole = pl.BlockSpec(pieces[0].shape, lambda g: (0, 0, 0))
    return pl.pallas_call(
        transform_kernel,
        grid=(8,),
        out_shape=(
            jax.ShapeDtypeStruct((2, rows, width), BF16),
            jax.ShapeDtypeStruct((rows, width), BF16),
            jax.ShapeDtypeStruct((rows, width), F32),
        ),
        in_specs=[pl.BlockSpec((half, depth), lambda g: (g, 0))] + [whole] * 4,
        out_specs=[
            pl.BlockSpec((1, half, width), lambda g: (jnp.minimum(g // 2, 1), jnp.where(g < 4, g % 2, 1), 0)),
            pl.BlockSpec((half, width), lambda g: (jnp.clip(g - 4, 0, 1), 0)),
            pl.BlockSpec((half, width), lambda g: (jnp.maximum(g - 6, 0), 0)),
        ],
        cost_estimate=pl.CostEstimate(
            flops=2 * span * depth * width,
            bytes_accessed=2 * span * depth + 2 * depth * width + 3 * span * width,
            transcendentals=0,
        ),
        name="transform",
    )(table, *pieces)


def gather_rows_kernel(ids, own, near, far, direct, *outs):
    rows = outs[0].shape[0]
    for m, out in enumerate(outs):
        here = pl.ds(pl.multiple_of(ids[m] * rows, rows), rows)
        total = own[here, :] + direct[here, :].astype(F32)
        total = total + near[here, :].astype(F32) + far[here, :].astype(F32)
        out[...] = total.astype(BF16)


def gather_rows(ids, own, near, far, direct):
    rows, width = own.shape
    piece = jax.ShapeDtypeStruct((rows // 4, width), BF16)
    whole = pl.BlockSpec((rows, width), lambda g, ids: (0, 0))
    return pl.pallas_call(
        gather_rows_kernel,
        out_shape=(piece,) * 4,
        grid_spec=pltpu.PrefetchScalarGridSpec(
            num_scalar_prefetch=1,
            grid=(1,),
            in_specs=[whole] * 4,
            out_specs=[pl.BlockSpec(piece.shape, lambda g, ids: (0, 0))] * 4,
        ),
        cost_estimate=pl.CostEstimate(
            flops=3 * rows * width, bytes_accessed=12 * rows * width, transcendentals=0
        ),
        name="gather_rows",
    )(ids, own, near, far, direct)


def project_kernel(scale, ids, *refs):
    pieces, gates, weights = refs[:4], refs[4:8], refs[8:12]
    carried, out = refs[12], refs[13]
    total = carried[...]
    for piece, gate, weight in zip(pieces, gates, weights):
        mixed = piece[...].astype(F32) * scale
        gated = (mixed * gate[...].astype(F32)).astype(BF16)
        total = total + jnp.dot(gated, weight[...], preferred_element_type=F32)
    out[...] = total


def project(ids, pieces, gate, weights, carried, offset, scale):
    rows, width = pieces[0].shape
    outs = weights.shape[1]
    first = offset // width

    def gate_piece(m):
        return pl.BlockSpec((rows, width), lambda g, ids: (0, first + ids[m]))

    def weight_piece(m):
        return pl.BlockSpec((width, outs), lambda g, ids: (first + ids[m], 0))

    whole = pl.BlockSpec((rows, width), lambda g, ids: (0, 0))
    sums = pl.BlockSpec((rows, outs), lambda g, ids: (0, 0))
    return pl.pallas_call(
        lambda *refs: project_kernel(scale, *refs),
        out_shape=jax.ShapeDtypeStruct((rows, outs), F32),
        grid_spec=pltpu.PrefetchScalarGridSpec(
            num_scalar_prefetch=1,
            grid=(1,),
            in_specs=[whole] * 4
            + [gate_piece(m) for m in range(4)]
            + [weight_piece(m) for m in range(4)]
            + [sums],
            out_specs=sums,
        ),
        cost_estimate=pl.CostEstimate(
            flops=8 * rows * width * outs, bytes_accessed=16 * rows * width + 8 * width * outs, transcendentals=0
        ),
        name="project",
    )(ids, *pieces, *([gate] * 4), *([weights] * 4), carried)


def attend_kernel(score_scale, ids, query, *refs):
    blocks, out = refs[:-1], refs[-1]
    rows, head = query.shape
    plane, query_block = ids[4], ids[5]
    query_pos = query_block * rows + lax.broadcasted_iota(jnp.int32, (rows, rows), 0)
    local = lax.broadcasted_iota(jnp.int32, (rows, rows), 1)
    scores, values = [], []
    for m in range(4):
        for back in range(PLANES):
            if back == 0:
                block = blocks[m][...]
            else:
                block = blocks[4 + m][back - 1]
            key_block = (plane - back) * 4 + ids[m]
            allowed = (key_block * rows + local <= query_pos) & (back <= plane)
            part = lax.dot_general(
                query[...], block[:, :head], (((1,), (1,)), ((), ())), preferred_element_type=F32
            )
            scores.append(jnp.where(allowed, part * score_scale, FLOOR))
            values.append(block[:, head:])
    top = scores[0]
    for part in scores[1:]:
        top = jnp.maximum(top, part)
    top = jnp.max(top, axis=1, keepdims=True)
    sums = None
    weighted = None
    for part, value in zip(scores, values):
        weight = jnp.exp(part - top)
        term = jnp.dot(weight.astype(BF16), value, preferred_element_type=F32)
        sums = weight if sums is None else sums + weight
        weighted = term if weighted is None else weighted + term
    totals = jnp.sum(sums, axis=1, keepdims=True)
    out[...] = (weighted / totals).astype(BF16)


def attend(ids, query, here, lower, score_scale):
    rows, head = query.shape
    flat = pl.BlockSpec(here[0].shape, lambda g, ids: (0, 0))
    stack = pl.BlockSpec(lower[0].shape, lambda g, ids: (0, 0, 0))
    return pl.pallas_call(
        lambda *refs: attend_kernel(score_scale, *refs),
        out_shape=jax.ShapeDtypeStruct((rows, head), BF16),
        grid_spec=pltpu.PrefetchScalarGridSpec(
            num_scalar_prefetch=1,
            grid=(1,),
            in_specs=[pl.BlockSpec((rows, head), lambda g, ids: (0, 0))] + [flat] * 4 + [stack] * 4,
            out_specs=pl.BlockSpec((rows, head), lambda g, ids: (0, 0)),
        ),
        cost_estimate=pl.CostEstimate(
            flops=64 * rows * rows * head, bytes_accessed=64 * rows * head, transcendentals=16 * rows * rows
        ),
        name="attend",
    )(ids, query, *here, *lower)


def make_table(plane, slots, ids, freqs, rows, span):
    freq_ids = jnp.arange(freqs, dtype=jnp.int32)
    row_ids = jnp.arange(rows, dtype=jnp.int32)
    fine = 16
    coarse_ids = jnp.arange(rows // fine, dtype=jnp.int32) * fine
    fine_ids = jnp.arange(fine, dtype=jnp.int32)
    coarse = unit_circle(coarse_ids[:, None] * freq_ids[None, :], span)
    small = unit_circle(fine_ids[:, None] * freq_ids[None, :], span)
    by_source = unit_circle(((plane * 4 + ids[:4]) * freqs % span)[:, None] * row_ids[None, :], span)
    by_slot = unit_circle((slots * rows)[:, None] * freq_ids[None, :], span)
    coarse, small, by_source, by_slot = lax.optimization_barrier((coarse, small, by_source, by_slot))
    base = times(
        tuple(part[:, None, :] for part in coarse), tuple(part[None, :, :] for part in small)
    )
    base = tuple(part.reshape(rows, 1, freqs) for part in base)
    turned = times(base, tuple(part.T[:, :, None] for part in by_source))
    turned = lax.optimization_barrier(turned)
    slot_re, slot_im = by_slot
    first = jnp.stack([slot_re, -slot_im], axis=1)[:, None, None]
    second = jnp.stack([-slot_im, -slot_re], axis=1)[:, None, None]
    table = first * turned[0][None, :, :, None, :] + second * turned[1][None, :, :, None, :]
    return table.astype(BF16).reshape(4 * rows, 8 * freqs)


def per_plane(signal_spectrum, filter_spectrum, output_gate, projection):
    axis_count = lax.axis_size("ctx")
    me = lax.axis_index("ctx")
    rows_dev, channels = output_gate.shape
    freqs_dev = signal_spectrum.shape[1]
    span = axis_count * freqs_dev
    head = projection.shape[1] // 3
    plane, spot = me // 4, me % 4
    ids = jnp.stack([spot, spot ^ 1, spot ^ 2, spot ^ 3, plane, me]).astype(jnp.int32)
    outer_low = plane < 2
    slots = jnp.stack(
        [
            jnp.where(outer_low, 2, 1),
            jnp.where(outer_low, 3, 0),
            plane ^ 1,
            plane,
        ]
    ).astype(jnp.int32)
    table = make_table(plane, slots, ids, freqs_dev, 4 * rows_dev, span)

    def among(pairs):
        return [(a * 4 + s, b * 4 + s) for a, b in pairs for s in range(4)]

    def swap(array, m):
        return lax.ppermute(array, "ctx", [(i, i ^ m) for i in range(axis_count)])

    unit = channels // 4 // sum(CHUNKS)
    widths = [unit * c for c in CHUNKS]
    offsets = [4 * sum(widths[:i]) for i in range(len(widths))]
    scale = 1.0 / math.sqrt(span)
    packed = jnp.zeros((rows_dev, 3 * head), F32)
    previous = None
    for width, offset in zip(widths, offsets):
        pieces = products(ids, signal_spectrum, filter_spectrum, offset, width)
        if previous is not None:
            pieces, previous = lax.optimization_barrier((pieces, previous))
        received = [swap(pieces[2], 2), swap(pieces[3], 3), swap(pieces[1], 1)]
        spectra = (pieces[0], received[2], received[0], received[1])
        previous = spectra
        across, direct, own = transform(table, spectra)
        handed = lax.ppermute(across, "ctx", among([(0, 1), (3, 2)]))
        direct = lax.ppermute(direct, "ctx", among([(0, 1), (1, 0), (2, 3), (3, 2)]))
        near = (across[0].astype(F32) + handed[0].astype(F32)).astype(BF16)
        far = (across[1].astype(F32) + handed[1].astype(F32)).astype(BF16)
        far = lax.ppermute(far, "ctx", among([(1, 3), (2, 0)]))
        near = lax.ppermute(near, "ctx", among([(1, 2), (2, 1)]))
        mine = gather_rows(ids, own, near, far, direct)
        mixed = (mine[0], swap(mine[1], 1), swap(mine[2], 2), swap(mine[3], 3))
        packed = project(ids, mixed, output_gate, projection, packed, offset, scale)

    packed = packed.astype(BF16)
    query, pairs = packed[:, :head], packed[:, head:]
    lower = jnp.stack(
        [
            lax.ppermute(pairs, "ctx", among([(p, p + back) for p in range(PLANES - back)]))
            for back in range(1, PLANES)
        ]
    )
    here = (pairs, swap(pairs, 1), swap(pairs, 2), swap(pairs, 3))
    below = (lower, swap(lower, 1), swap(lower, 2), swap(lower, 3))
    return attend(ids, query, here, below, 1.0 / math.sqrt(head))


def across_sources(pieces, span_total):
    sources, freq_count = pieces.shape[2], pieces.shape[3]
    form = "ud,cdp->cup"
    ordinal = jnp.arange(sources, dtype=jnp.int32)
    cos_table, sin_table = unit_circle(ordinal[:, None] * ordinal[None, :], sources)
    cos_table, sin_table = cos_table.astype(BF16), sin_table.astype(BF16)

    def turn(table, part):
        return jnp.einsum(form, table, part, preferred_element_type=F32)

    middle = (
        turn(cos_table, pieces[0]) - turn(sin_table, pieces[1]),
        turn(sin_table, pieces[0]) + turn(cos_table, pieces[1]),
    )
    freq_ids = jnp.arange(freq_count, dtype=jnp.int32)
    turns = unit_circle(ordinal[:, None] * freq_ids[None, :], span_total)
    return times(middle, turns)


def across_freqs(pieces, out_rows, freq_count, span_total):
    row_ids = jnp.arange(out_rows, dtype=jnp.int32)
    freq_ids = jnp.arange(freq_count, dtype=jnp.int32)
    cos_table, sin_table = unit_circle(row_ids[:, None] * freq_ids[None, :], freq_count)
    form = "vp,cup->vuc"
    result = jnp.einsum(form, cos_table.astype(BF16), pieces[0].astype(BF16), preferred_element_type=F32)
    result = result - jnp.einsum(
        form, sin_table.astype(BF16), pieces[1].astype(BF16), preferred_element_type=F32
    )
    return result * (1.0 / math.sqrt(span_total))


def per_device(signal_spectrum, filter_spectrum, output_gate, projection):
    axis_count = lax.axis_size("ctx")
    me_index = lax.axis_index("ctx")
    rows_dev = output_gate.shape[0]
    freqs_dev = signal_spectrum.shape[1]
    span_total = axis_count * freqs_dev
    head = projection.shape[1] // 3
    query_pos = me_index * rows_dev + jnp.arange(rows_dev, dtype=jnp.int32)
    signal = signal_spectrum.astype(F32)
    kernel = filter_spectrum.astype(F32)
    product = jnp.stack(times(signal, kernel)).astype(BF16)
    chan_count = product.shape[2] // axis_count
    turned = jnp.swapaxes(product, 1, 2)
    gathered = lax.all_to_all(turned, "ctx", split_axis=1, concat_axis=2, tiled=True)
    pieces = gathered.reshape(2, chan_count, axis_count, freqs_dev)
    spread = across_sources(pieces, span_total)
    mixed_rows = across_freqs(spread, rows_dev, freqs_dev, span_total).astype(BF16)
    mixed_rows = lax.all_to_all(
        mixed_rows.reshape(axis_count, rows_dev, chan_count),
        "ctx",
        split_axis=0,
        concat_axis=2,
        tiled=True,
    ).reshape(rows_dev, -1)
    gated = (mixed_rows.astype(F32) * output_gate.astype(F32)).astype(BF16)
    packed = jnp.dot(gated, projection, preferred_element_type=F32).astype(BF16)
    query_rows, pairs = packed[:, :head], packed[:, head:]
    score_scale = 1.0 / math.sqrt(head)
    top_query = jnp.max(query_pos)

    def absorb_block(carried, key_part, value_part, first_key):
        key_index = first_key + jnp.arange(key_part.shape[0], dtype=jnp.int32)

        def update(current):
            running_max, totals, weighted = current
            scores = score_scale * jnp.einsum(
                "qh,kh->qk", query_rows, key_part, preferred_element_type=F32
            )
            allowed = key_index[None, :] <= query_pos[:, None]
            scores = jnp.where(allowed, scores, FLOOR)
            new_max = jnp.maximum(running_max, jnp.max(scores, axis=1))
            exponents = jnp.where(allowed, jnp.exp(scores - new_max[:, None]), 0.0)
            factor = jnp.exp(running_max - new_max)
            totals = totals * factor + jnp.sum(exponents, axis=1)
            weighted = weighted * factor[:, None] + jnp.dot(
                exponents.astype(BF16), value_part, preferred_element_type=F32
            )
            return (new_max, totals, weighted)

        return lax.cond(jnp.min(key_index) > top_query, lambda current: current, update, carried)

    every = lax.all_gather(pairs, "ctx", axis=0, tiled=True)
    key_total = every.shape[0]
    block_rows = 2048 if key_total % 2048 == 0 else key_total
    blocks = every.reshape(key_total // block_rows, block_rows, -1)
    firsts = block_rows * jnp.arange(blocks.shape[0], dtype=jnp.int32)

    def step_block(current, inputs):
        block, first = inputs
        return absorb_block(current, block[:, :head], block[:, head:], first), None

    initial = (
        jnp.full((rows_dev,), FLOOR, F32),
        jnp.zeros((rows_dev,), F32),
        jnp.zeros((rows_dev, head), F32),
    )
    (running_max, totals, weighted), _ = lax.scan(step_block, initial, (blocks, firsts))
    return (weighted / totals[:, None]).astype(BF16)


def solution(mesh):
    in_specs = (
        P(None, ("groups", "ctx"), None),
        P(None, "ctx", None),
        P(("groups", "ctx"), None),
        P(),
    )
    out_specs = P(("groups", "ctx"), None)
    body = per_plane if mesh.shape["ctx"] == 4 * PLANES else per_device
    return jax.shard_map(
        body, mesh=mesh, in_specs=in_specs, out_specs=out_specs, check_vma=False
    )
```

```python
import math

import jax
import jax.numpy as jnp
from jax import lax
from jax.experimental import pallas as pl
from jax.experimental.pallas import tpu as pltpu
from jax.sharding import PartitionSpec as P

TWO_PI = 2.0 * math.pi
FLOOR = -1e30
BF16 = jnp.bfloat16
F32 = jnp.float32
PLANES = 4
CHUNKS = 4


def unit_circle(numerator, modulus):
    phases = TWO_PI / modulus * (numerator % modulus).astype(F32)
    return jnp.cos(phases), jnp.sin(phases)


def times(left, right):
    return left[0] * right[0] - left[1] * right[1], left[0] * right[1] + left[1] * right[0]


def product_kernel(count, ids, *refs):
    signals, filters, outs = refs[:4], refs[4:8], refs[8:]
    step = pl.program_id(0)
    for m, (signal, kernel) in enumerate(zip(signals, filters)):
        s_re, s_im = signal[0].astype(F32), signal[1].astype(F32)
        k_re, k_im = kernel[0].astype(F32), kernel[1].astype(F32)
        real = (s_re * k_re - s_im * k_im).astype(BF16)
        imag = (s_re * k_im + s_im * k_re).astype(BF16)
        for chunk in range(count):

            @pl.when(step == chunk)
            def _():
                outs[4 * chunk + m][0] = real
                outs[4 * chunk + m][1] = imag


def products(ids, signal, kernel, first, count, width):
    freqs = signal.shape[1]
    stride = signal.shape[2] // (4 * width)

    def piece(m):
        return pl.BlockSpec((2, freqs, width), lambda g, ids: (0, 0, ids[m] * stride + first + g))

    out = jax.ShapeDtypeStruct((2, freqs, width), BF16)
    outs = pl.pallas_call(
        lambda *refs: product_kernel(count, *refs),
        out_shape=(out,) * (4 * count),
        grid_spec=pltpu.PrefetchScalarGridSpec(
            num_scalar_prefetch=1,
            grid=(count,),
            in_specs=[piece(m) for m in range(4)] * 2,
            out_specs=[pl.BlockSpec((2, freqs, width), lambda g, ids: (0, 0, 0))] * (4 * count),
        ),
        cost_estimate=pl.CostEstimate(
            flops=24 * freqs * width * count, bytes_accessed=48 * freqs * width * count, transcendentals=0
        ),
        name="products",
    )(ids, *([signal] * 4), *([kernel] * 4))
    return [outs[4 * chunk : 4 * chunk + 4] for chunk in range(count)]


def split_kernel(ids, *refs):
    for source, out in zip(refs[:4], refs[4:]):
        out[...] = source[...]


def split_gate(ids, gate):
    rows, channels = gate.shape
    width = channels // 4

    def piece(m):
        return pl.BlockSpec((rows, width), lambda g, ids: (0, ids[m]))

    return pl.pallas_call(
        split_kernel,
        out_shape=(jax.ShapeDtypeStruct((rows, width), gate.dtype),) * 4,
        grid_spec=pltpu.PrefetchScalarGridSpec(
            num_scalar_prefetch=1,
            grid=(1,),
            in_specs=[piece(m) for m in range(4)],
            out_specs=[pl.BlockSpec((rows, width), lambda g, ids: (0, 0))] * 4,
        ),
        cost_estimate=pl.CostEstimate(flops=0, bytes_accessed=4 * rows * channels, transcendentals=0),
        name="split_gate",
    )(ids, *([gate] * 4))


def table_kernel(coarse, small, by_source, by_slot, out, turned_re, turned_im):
    step = pl.program_id(0)
    rows, freqs = out.shape[0], small.shape[2]
    fine = small.shape[1]

    @pl.when(step == 0)
    def _():
        for a in range(rows // fine):
            here = slice(a * fine, (a + 1) * fine)
            base_re = coarse[0, a : a + 1] * small[0] - coarse[1, a : a + 1] * small[1]
            base_im = coarse[0, a : a + 1] * small[1] + coarse[1, a : a + 1] * small[0]
            for m in range(4):
                side_re = by_source[0, here, m : m + 1]
                side_im = by_source[1, here, m : m + 1]
                cols = slice(m * freqs, (m + 1) * freqs)
                turned_re[here, cols] = base_re * side_re - base_im * side_im
                turned_im[here, cols] = base_re * side_im + base_im * side_re

    slot_re = by_slot[0, pl.ds(step, 1), :]
    slot_im = by_slot[1, pl.ds(step, 1), :]
    for m in range(4):
        cols = slice(m * freqs, (m + 1) * freqs)
        re, im = turned_re[:, cols], turned_im[:, cols]
        out[:, 2 * m * freqs : (2 * m + 1) * freqs] = (re * slot_re - im * slot_im).astype(BF16)
        out[:, (2 * m + 1) * freqs : (2 * m + 2) * freqs] = (-(re * slot_im + im * slot_re)).astype(BF16)


def make_table(plane, slots, ids, freqs, rows, span):
    freq_ids = jnp.arange(freqs, dtype=jnp.int32)
    fine = 16
    quarter = rows // 4
    starts = jnp.arange(quarter // fine, dtype=jnp.int32) * fine
    coarse_ids = (ids[:4, None] * quarter + starts[None, :]).reshape(-1)
    row_ids = (ids[:4, None] * quarter + jnp.arange(quarter, dtype=jnp.int32)[None, :]).reshape(-1)
    fine_ids = jnp.arange(fine, dtype=jnp.int32)
    coarse = jnp.stack(unit_circle(coarse_ids[:, None] * freq_ids[None, :], span))
    small = jnp.stack(unit_circle(fine_ids[:, None] * freq_ids[None, :], span))
    by_slot = jnp.stack(unit_circle((slots * rows)[:, None] * freq_ids[None, :], span))
    source_ids = (plane * 4 + ids[:4]) * freqs
    by_source = jnp.stack(unit_circle(row_ids[:, None] * source_ids[None, :], span))
    args = (coarse, small, by_source, by_slot)
    return pl.pallas_call(
        table_kernel,
        grid=(4,),
        out_shape=jax.ShapeDtypeStruct((4 * rows, 8 * freqs), BF16),
        in_specs=[pl.BlockSpec(arg.shape, lambda g: (0, 0, 0)) for arg in args],
        out_specs=pl.BlockSpec((rows, 8 * freqs), lambda g: (g, 0)),
        scratch_shapes=[pltpu.VMEM((rows, 4 * freqs), F32)] * 2,
        cost_estimate=pl.CostEstimate(
            flops=120 * rows * freqs, bytes_accessed=64 * rows * freqs, transcendentals=0
        ),
        name="table",
    )(*args)


def transform_kernel(table, p0, p1, p2, p3, out_a, out_b, out_own, held, data, low, high, in_sems, data_sems, out_sems):
    rows = high.shape[0]
    blocks = held.shape[0] // rows * 2
    half = rows // 2
    depth = data.shape[1] * data.shape[2]
    width = data.shape[3]

    def load(block):
        here = slice(block * half, (block + 1) * half)
        return pltpu.make_async_copy(table.at[here], held.at[here], in_sems.at[block])

    fetches = [pltpu.make_async_copy(piece, data.at[m], data_sems.at[m]) for m, piece in enumerate((p0, p1, p2, p3))]
    load(0).start()
    for fetch in fetches:
        fetch.start()
    for block in range(1, blocks):
        load(block).start()
    for fetch in fetches:
        fetch.wait()
    stores = []
    for block in range(blocks):
        load(block).wait()
        here = slice(block * half, (block + 1) * half)
        total = None
        for m in range(4):
            term = jnp.dot(
                held[here, m * depth : (m + 1) * depth],
                data[m].reshape(depth, width),
                preferred_element_type=F32,
            )
            total = term if total is None else total + term
        slot, part = block // 2, slice(block % 2 * half, (block % 2 + 1) * half)
        if slot < 3:
            low[here] = total.astype(BF16)
            target = out_a.at[slot, part] if slot < 2 else out_b.at[part]
            store = pltpu.make_async_copy(low.at[here], target, out_sems.at[block])
        else:
            high[part] = total
            store = pltpu.make_async_copy(high.at[part], out_own.at[part], out_sems.at[block])
        store.start()
        stores.append(store)
    for store in stores:
        store.wait()


def transform(table, pieces):
    width = pieces[0].shape[2]
    span, depth = table.shape
    rows = span // 4
    anywhere = pl.BlockSpec(memory_space=pl.ANY)
    return pl.pallas_call(
        transform_kernel,
        out_shape=(
            jax.ShapeDtypeStruct((2, rows, width), BF16),
            jax.ShapeDtypeStruct((rows, width), BF16),
            jax.ShapeDtypeStruct((rows, width), F32),
        ),
        in_specs=[anywhere] * 5,
        out_specs=[anywhere] * 3,
        scratch_shapes=[
            pltpu.VMEM((span, depth), BF16),
            pltpu.VMEM((4,) + pieces[0].shape, BF16),
            pltpu.VMEM((3 * rows, width), BF16),
            pltpu.VMEM((rows, width), F32),
            pltpu.SemaphoreType.DMA((8,)),
            pltpu.SemaphoreType.DMA((4,)),
            pltpu.SemaphoreType.DMA((8,)),
        ],
        cost_estimate=pl.CostEstimate(
            flops=2 * span * depth * width,
            bytes_accessed=2 * span * depth + 2 * depth * width + 3 * span * width,
            transcendentals=0,
        ),
        name="transform",
    )(table, *pieces)


def project_kernel(scale, first, last, *refs):
    own, near, far, direct = refs[1:5]
    gates, weight = refs[5:9], refs[9]
    carried = None if first else refs[10]
    outs = refs[10 if first else 11 :]
    rows = gates[0].shape[0]
    for m, gate in enumerate(gates):
        here = slice(m * rows, (m + 1) * rows)
        mixed = own[here, :] + direct[here, :].astype(F32)
        mixed = mixed + near[here, :].astype(F32) + far[here, :].astype(F32)
        gated = (mixed * scale * gate[...].astype(F32)).astype(BF16)
        total = jnp.dot(gated, weight[...], preferred_element_type=F32)
        if not first:
            total = total + carried[here, :]
        if last:
            outs[m][...] = total.astype(outs[m].dtype)
        else:
            outs[0][here, :] = total


def project(ids, parts, gates, weights, carried, chunk, scale, last):
    rows, width = parts[0].shape
    outs = weights.shape[1]
    stride = weights.shape[0] // (4 * width)
    whole = pl.BlockSpec((rows, width), lambda g, ids: (0, 0))
    gate = pl.BlockSpec((rows // 4, width), lambda g, ids: (0, chunk))
    sums = pl.BlockSpec((rows, outs), lambda g, ids: (0, 0))
    quarter = pl.BlockSpec((rows // 4, outs), lambda g, ids: (0, 0))
    if last:
        shapes = tuple(
            jax.ShapeDtypeStruct((rows // 4, outs), F32 if m == 0 else BF16) for m in range(4)
        )
        out_specs = [quarter] * 4
    else:
        shapes = jax.ShapeDtypeStruct((rows, outs), F32)
        out_specs = sums
    extra = () if carried is None else (carried,)
    return pl.pallas_call(
        lambda *refs: project_kernel(scale, carried is None, last, *refs),
        out_shape=shapes,
        grid_spec=pltpu.PrefetchScalarGridSpec(
            num_scalar_prefetch=1,
            grid=(1,),
            in_specs=[whole] * 4
            + [gate] * 4
            + [pl.BlockSpec((width, outs), lambda g, ids: (ids[0] * stride + chunk, 0))]
            + [sums] * len(extra),
            out_specs=out_specs,
        ),
        cost_estimate=pl.CostEstimate(
            flops=2 * rows * width * outs,
            bytes_accessed=12 * rows * width + 2 * width * outs + 8 * rows * outs,
            transcendentals=0,
        ),
        name="project",
    )(ids, *parts, *gates, weights, *extra)


def settle_kernel(own, r1, r2, r3, query, pairs):
    total = own[...] + r1[...].astype(F32) + r2[...].astype(F32) + r3[...].astype(F32)
    head = query.shape[1]
    query[...] = total[:, :head].astype(BF16)
    pairs[...] = total[:, head:].astype(BF16)


def settle(parts):
    rows, outs = parts[0].shape
    head = outs // 3
    return pl.pallas_call(
        settle_kernel,
        out_shape=(
            jax.ShapeDtypeStruct((rows, head), BF16),
            jax.ShapeDtypeStruct((rows, 2 * head), BF16),
        ),
        cost_estimate=pl.CostEstimate(flops=3 * rows * outs, bytes_accessed=12 * rows * outs, transcendentals=0),
        name="settle",
    )(*parts)


def attend_kernel(score_scale, ids, *refs):
    queries, blocks, outs = refs[:4], refs[4:8], refs[8:]
    rows, head = queries[0].shape
    spot, plane = ids[0], ids[4]
    query_row = lax.broadcasted_iota(jnp.int32, (rows, rows), 0)
    key_row = lax.broadcasted_iota(jnp.int32, (rows, rows), 1)
    stacked = jnp.concatenate([query[...] for query in queries], axis=0)
    scores = [
        score_scale
        * lax.dot_general(
            stacked, block[:, :head], (((1,), (1,)), ((), ())), preferred_element_type=F32
        )
        for block in blocks
    ]
    for m, out in enumerate(outs):
        here = slice(m * rows, (m + 1) * rows)
        parts, masks = [], []
        for back in range(PLANES):
            if back > 0:
                allowed = jnp.broadcast_to(plane, (rows, rows)) >= back
            elif m > 0:
                allowed = jnp.broadcast_to(spot, (rows, rows)) < ids[m]
            else:
                allowed = key_row <= query_row
            masks.append(allowed)
            parts.append(jnp.where(allowed, scores[back][here, :], FLOOR))
        top = jnp.maximum(jnp.maximum(parts[0], parts[1]), jnp.maximum(parts[2], parts[3]))
        top = jnp.max(top, axis=1, keepdims=True)
        weighted, sums = None, None
        for part, allowed, block in zip(parts, masks, blocks):
            weight = jnp.where(allowed, jnp.exp(part - top), 0.0)
            term = jnp.dot(weight.astype(BF16), block[:, head:], preferred_element_type=F32)
            weighted = term if weighted is None else weighted + term
            sums = weight if sums is None else sums + weight
        total = jnp.sum(sums, axis=1, keepdims=True)
        stats = jnp.where(key_row < 4, top, total)
        out[:rows, :] = weighted
        out[rows:, :] = jnp.transpose(stats)[:8, :]


def attend(ids, queries, blocks, score_scale):
    rows, head = queries[0].shape
    row_spec = pl.BlockSpec((rows, head), lambda g, ids: (0, 0))
    pair_spec = pl.BlockSpec((rows, 2 * head), lambda g, ids: (0, 0))
    return pl.pallas_call(
        lambda *refs: attend_kernel(score_scale, *refs),
        out_shape=(jax.ShapeDtypeStruct((rows + 8, head), F32),) * 4,
        grid_spec=pltpu.PrefetchScalarGridSpec(
            num_scalar_prefetch=1,
            grid=(1,),
            in_specs=[row_spec] * 4 + [pair_spec] * 4,
            out_specs=[pl.BlockSpec((rows + 8, head), lambda g, ids: (0, 0))] * 4,
        ),
        cost_estimate=pl.CostEstimate(
            flops=64 * rows * rows * head, bytes_accessed=40 * rows * head, transcendentals=16 * rows * rows
        ),
        name="attend",
    )(ids, *queries, *blocks)


def combine_kernel(*refs):
    parts, out = refs[:4], refs[4]
    rows, head = out.shape
    tops = [jnp.transpose(jnp.broadcast_to(part[rows : rows + 1, :], (rows, head))) for part in parts]
    sums = [jnp.transpose(jnp.broadcast_to(part[rows + 4 : rows + 5, :], (rows, head))) for part in parts]
    top = jnp.maximum(jnp.maximum(tops[0], tops[1]), jnp.maximum(tops[2], tops[3]))
    weighted, total = None, None
    for part, one_top, one_sum in zip(parts, tops, sums):
        factor = jnp.exp(one_top - top)
        weighted = part[:rows, :] * factor + (0.0 if weighted is None else weighted)
        total = one_sum * factor + (0.0 if total is None else total)
    out[...] = (weighted / total).astype(BF16)


def combine(parts):
    rows, head = parts[0].shape[0] - 8, parts[0].shape[1]
    return pl.pallas_call(
        combine_kernel,
        out_shape=jax.ShapeDtypeStruct((rows, head), BF16),
        cost_estimate=pl.CostEstimate(
            flops=20 * rows * head, bytes_accessed=18 * rows * head, transcendentals=4 * rows * head
        ),
        name="combine",
    )(*parts)


def per_plane(signal_spectrum, filter_spectrum, output_gate, projection):
    axis_count = lax.axis_size("ctx")
    me = lax.axis_index("ctx")
    rows_dev, channels = output_gate.shape
    freqs_dev = signal_spectrum.shape[1]
    span = axis_count * freqs_dev
    head = projection.shape[1] // 3
    width = channels // (4 * CHUNKS)
    plane, spot = me // 4, me % 4
    ids = jnp.stack([spot, spot ^ 1, spot ^ 2, spot ^ 3, plane, me]).astype(jnp.int32)
    low = plane < 2
    slots = jnp.stack([jnp.where(low, 2, 1), jnp.where(low, 3, 0), plane ^ 1, plane]).astype(jnp.int32)

    def among(pairs):
        return [(a * 4 + s, b * 4 + s) for a, b in pairs for s in range(4)]

    def swap(array, m):
        return lax.ppermute(array, "ctx", [(i, i ^ m) for i in range(axis_count)])

    def exchange(pieces):
        second, third = swap(pieces[2], 2), swap(pieces[3], 3)
        return (pieces[0], swap(pieces[1], 1), second, third)

    scale = 1.0 / math.sqrt(span)
    pieces = products(ids, signal_spectrum, filter_spectrum, 0, 1, width)
    table = make_table(plane, slots, ids, freqs_dev, 4 * rows_dev, span)
    pieces += products(ids, signal_spectrum, filter_spectrum, 1, CHUNKS - 1, width)
    gate_pieces = split_gate(ids, output_gate)
    waiting, gates, previous = [], None, None
    for chunk in range(CHUNKS):
        here = pieces[chunk]
        if previous is not None:
            here, previous = lax.optimization_barrier((here, previous))
        spectra = exchange(here)
        previous = spectra
        if chunk == 1:
            gate_pieces, previous = lax.optimization_barrier((gate_pieces, previous))
            gates = exchange(gate_pieces)
            previous = (spectra, gates)
        across, direct, own = transform(table, spectra)
        handed = lax.ppermute(across, "ctx", among([(0, 1), (3, 2)]))
        direct = lax.ppermute(direct, "ctx", among([(0, 1), (1, 0), (2, 3), (3, 2)]))
        near = (across[0].astype(F32) + handed[0].astype(F32)).astype(BF16)
        far = (across[1].astype(F32) + handed[1].astype(F32)).astype(BF16)
        far = lax.ppermute(far, "ctx", among([(1, 3), (2, 0)]))
        near = lax.ppermute(near, "ctx", among([(1, 2), (2, 1)]))
        waiting.append((own, near, far, direct))

    packed = None
    for chunk, parts in enumerate(waiting):
        packed = project(ids, parts, gates, projection, packed, chunk, scale, chunk == CHUNKS - 1)
    query, pairs = settle(exchange(packed))
    blocks = (pairs,) + tuple(
        lax.ppermute(pairs, "ctx", among([(p, p + back) for p in range(PLANES - back)]))
        for back in range(1, PLANES)
    )
    queries = exchange((query,) * 4)
    return combine(exchange(attend(ids, queries, blocks, 1.0 / math.sqrt(head))))


def across_sources(pieces, span_total):
    sources, freq_count = pieces.shape[2], pieces.shape[3]
    form = "ud,cdp->cup"
    ordinal = jnp.arange(sources, dtype=jnp.int32)
    cos_table, sin_table = unit_circle(ordinal[:, None] * ordinal[None, :], sources)
    cos_table, sin_table = cos_table.astype(BF16), sin_table.astype(BF16)

    def turn(table, part):
        return jnp.einsum(form, table, part, preferred_element_type=F32)

    middle = (
        turn(cos_table, pieces[0]) - turn(sin_table, pieces[1]),
        turn(sin_table, pieces[0]) + turn(cos_table, pieces[1]),
    )
    freq_ids = jnp.arange(freq_count, dtype=jnp.int32)
    turns = unit_circle(ordinal[:, None] * freq_ids[None, :], span_total)
    return times(middle, turns)


def across_freqs(pieces, out_rows, freq_count, span_total):
    row_ids = jnp.arange(out_rows, dtype=jnp.int32)
    freq_ids = jnp.arange(freq_count, dtype=jnp.int32)
    cos_table, sin_table = unit_circle(row_ids[:, None] * freq_ids[None, :], freq_count)
    form = "vp,cup->vuc"
    result = jnp.einsum(form, cos_table.astype(BF16), pieces[0].astype(BF16), preferred_element_type=F32)
    result = result - jnp.einsum(
        form, sin_table.astype(BF16), pieces[1].astype(BF16), preferred_element_type=F32
    )
    return result * (1.0 / math.sqrt(span_total))


def per_device(signal_spectrum, filter_spectrum, output_gate, projection):
    axis_count = lax.axis_size("ctx")
    me_index = lax.axis_index("ctx")
    rows_dev = output_gate.shape[0]
    freqs_dev = signal_spectrum.shape[1]
    span_total = axis_count * freqs_dev
    head = projection.shape[1] // 3
    query_pos = me_index * rows_dev + jnp.arange(rows_dev, dtype=jnp.int32)
    signal = signal_spectrum.astype(F32)
    kernel = filter_spectrum.astype(F32)
    product = jnp.stack(times(signal, kernel)).astype(BF16)
    chan_count = product.shape[2] // axis_count
    turned = jnp.swapaxes(product, 1, 2)
    gathered = lax.all_to_all(turned, "ctx", split_axis=1, concat_axis=2, tiled=True)
    pieces = gathered.reshape(2, chan_count, axis_count, freqs_dev)
    spread = across_sources(pieces, span_total)
    mixed_rows = across_freqs(spread, rows_dev, freqs_dev, span_total).astype(BF16)
    mixed_rows = lax.all_to_all(
        mixed_rows.reshape(axis_count, rows_dev, chan_count),
        "ctx",
        split_axis=0,
        concat_axis=2,
        tiled=True,
    ).reshape(rows_dev, -1)
    gated = (mixed_rows.astype(F32) * output_gate.astype(F32)).astype(BF16)
    packed = jnp.dot(gated, projection, preferred_element_type=F32).astype(BF16)
    query_rows, pairs = packed[:, :head], packed[:, head:]
    score_scale = 1.0 / math.sqrt(head)
    top_query = jnp.max(query_pos)

    def absorb_block(carried, key_part, value_part, first_key):
        key_index = first_key + jnp.arange(key_part.shape[0], dtype=jnp.int32)

        def update(current):
            running_max, totals, weighted = current
            scores = score_scale * jnp.einsum(
                "qh,kh->qk", query_rows, key_part, preferred_element_type=F32
            )
            allowed = key_index[None, :] <= query_pos[:, None]
            scores = jnp.where(allowed, scores, FLOOR)
            new_max = jnp.maximum(running_max, jnp.max(scores, axis=1))
            exponents = jnp.where(allowed, jnp.exp(scores - new_max[:, None]), 0.0)
            factor = jnp.exp(running_max - new_max)
            totals = totals * factor + jnp.sum(exponents, axis=1)
            weighted = weighted * factor[:, None] + jnp.dot(
                exponents.astype(BF16), value_part, preferred_element_type=F32
            )
            return (new_max, totals, weighted)

        return lax.cond(jnp.min(key_index) > top_query, lambda current: current, update, carried)

    every = lax.all_gather(pairs, "ctx", axis=0, tiled=True)
    key_total = every.shape[0]
    block_rows = 2048 if key_total % 2048 == 0 else key_total
    blocks = every.reshape(key_total // block_rows, block_rows, -1)
    firsts = block_rows * jnp.arange(blocks.shape[0], dtype=jnp.int32)

    def step_block(current, inputs):
        block, first = inputs
        return absorb_block(current, block[:, :head], block[:, head:], first), None

    initial = (
        jnp.full((rows_dev,), FLOOR, F32),
        jnp.zeros((rows_dev,), F32),
        jnp.zeros((rows_dev, head), F32),
    )
    (running_max, totals, weighted), _ = lax.scan(step_block, initial, (blocks, firsts))
    return (weighted / totals[:, None]).astype(BF16)


def solution(mesh):
    in_specs = (
        P(None, ("groups", "ctx"), None),
        P(None, "ctx", None),
        P(("groups", "ctx"), None),
        P(),
    )
    out_specs = P(("groups", "ctx"), None)

    def body(signal_spectrum, filter_spectrum, output_gate, projection):
        devices = mesh.shape["ctx"]
        even = 4 * output_gate.shape[0] % devices == 0 and projection.shape[0] % (4 * 128 * CHUNKS) == 0
        fits = devices == 4 * PLANES and even
        form = per_plane if fits else per_device
        return form(signal_spectrum, filter_spectrum, output_gate, projection)

    return jax.shard_map(
        body, mesh=mesh, in_specs=in_specs, out_specs=out_specs, check_vma=False
    )
```
